32 devices in a mesh: tile: 8 (over z, core), layer: 4 (over y, x).
Axes of the slice: x: 2, y: 2, z: 4, core: 2. Of those that a mesh axis runs over, the one named last changes fastest.
Arguments:
- basis: float32 [8, 768, 32], P('tile'), may hold values from -0.21875 to 0.21875
- ranks: int32 [8], P('tile'), may hold values from 8 to 32
- cores: float32 [8, 8, 32, 32], P('tile', 'layer'), may hold values from -1.11 to 1.11
- diag: float32 [8, 768, 768], P('tile', 'layer'), may hold values from 0 to 9, as said below
Outputs:
- factors: float32 [1, 768, 768], P(None, 'layer')
- panel_basis: float32 [1, 768, 32], replicated
- schur_diag: float32 [8, 768, 768], P('tile', 'layer')
- schur_cores: float32 [8, 8, 32, 32], P('tile', 'layer')
The draws below stay inside these ranges and needn't reach their ends.
Inputs may be any that keep to these rules, and one draw needn't show every extreme that they name: `diag`: each tile is a Gaussian kernel of points in the unit cube plus a multiple of the identity, so symmetric positive definite.
All inputs are finite; a program needn't handle non-finite values.
Results may differ from the reference program's by a relative error of at most 0.0001.
Values sent between devices are 32-bit elements; how exact they have to be, the bound alone decides.
A program may use at most 64 MiB of HBM per device.

```python
import jax
import jax.numpy as jnp
from jax import lax

TS = 768
RMAX = 32
PANELS = 1
NT = 8


def draw_diag(key, part):
    points = jax.random.uniform(key, (NT, TS, 3), jnp.float32)
    spread = 0.25
    nugget = 8.0
    norms = jnp.sum(points * points, axis=-1)
    cross = jnp.einsum('tad,tbd->tab', points, points, precision=jax.lax.Precision.HIGHEST)
    dist = jnp.maximum(norms[:, :, None] + norms[:, None, :] - 2.0 * cross, 0.0)
    kernel = jnp.exp(-dist / (2.0 * spread * spread))
    return kernel + nugget * jnp.eye(TS, dtype=jnp.float32)[None]


def draw_cores(key, part):
    spread = 0.37
    values = jax.random.normal(key, (NT, NT, RMAX, RMAX), jnp.float32)
    values = jnp.clip(values, -3.0, 3.0) * spread
    return values


def set_ends(entries, own_key, least, high):
    place = [jax.random.randint(jax.random.fold_in(own_key, axis), (), 0, length) for axis, length in enumerate(entries.shape)]
    longest = entries.shape.index(max(entries.shape))
    next_to = place[:longest] + [(place[longest] + 1) % entries.shape[longest]] + place[longest + 1:]
    return entries.at[tuple(place)].set(least).at[tuple(next_to)].set(high)


def steps_of(rng, extent, split, low, high):
    level, own = 1.0, jax.random.fold_in(rng, 6)
    for dim, shards_of in split:
        steps = jnp.exp(jax.random.uniform(jax.random.fold_in(own, dim), (shards_of,), jnp.float32, low / len(split), high / len(split)))
        level = level * jnp.repeat(steps, extent[dim] // shards_of).reshape([-1 if axis == dim else 1 for axis in range(len(extent))])
    return level


def gaussian(key, shape, scale, limit, shards=(), kind=jnp.bfloat16):
    level = steps_of(key, shape, shards, -0.22, 0.18) if shards else 1.0
    values = jax.random.normal(key, shape, jnp.float32) * scale * level
    return jnp.minimum(jnp.maximum(values, -limit), limit).astype(kind)


def setup_inputs(seed: int = 0) -> dict:
    arg_keys = jax.random.split(jax.random.key(seed), 5)
    return {
        "basis": gaussian(arg_keys[0], (NT, TS, RMAX), TS ** -0.5, 0.21875, ((0, 8),), jnp.float32),
        "ranks": set_ends(jax.random.randint(arg_keys[1], (NT,), RMAX // 4, RMAX + 1), jax.random.fold_in(arg_keys[1], 1), RMAX // 4, RMAX).astype(jnp.int32),
        "cores": draw_cores(jax.random.fold_in(arg_keys[4], 71), 0),
        "diag": draw_diag(jax.random.fold_in(arg_keys[4], 71), 0),
    }


HI = lax.Precision.HIGHEST

def factor(tile, panel_u):
    lower = jnp.linalg.cholesky(tile)
    solved = lax.linalg.triangular_solve(lower, panel_u, left_side=True, lower=True)
    gram = jnp.dot(solved.T, solved, precision=HI)
    return (lower, solved, gram)

def reference(basis, ranks, cores, diag):
    keep = (jnp.arange(RMAX, dtype=jnp.int32)[None, :] < ranks[:, None]).astype(jnp.float32)
    masked = basis * keep[:, None, :]
    ids = jnp.arange(NT, dtype=jnp.int32)
    factors = []
    bases = []
    for panel in range(PANELS):
        lower, solved, gram = factor(diag[panel], masked[panel])
        factors.append(lower)
        bases.append(solved)
        column = cores[:, panel]
        coef = jnp.einsum('trs,su->tru', column, gram, precision=HI)
        inner = jnp.einsum('tru,tvu->trv', coef, column, precision=HI)
        partial_rows = jnp.einsum('tar,trv->tav', masked, inner, precision=HI)
        change = jnp.einsum('tav,tbv->tab', partial_rows, masked, precision=HI)
        diag = diag - jnp.where((ids > panel)[:, None, None], change, 0.0)
        pair = jnp.einsum('tru,cvu->tcrv', coef, column, precision=HI)
        live = (ids[:, None] > ids[None, :]) & (ids[None, :] > panel)
        cores = cores - jnp.where(live[:, :, None, None], pair, 0.0)
    return (jnp.stack(factors), jnp.stack(bases), diag, cores)
```

```python
import functools

import jax
import jax.numpy as jnp
from jax import lax
from jax.experimental import pallas as pl
from jax.experimental.pallas import tpu as pltpu
from jax.sharding import PartitionSpec as P

B = 128
S = 8
NEAR = 2


def split(a):
    high = a.astype(jnp.bfloat16)
    return high, (a - high.astype(jnp.float32)).astype(jnp.bfloat16)


def three(a, b, dims):
    ah, al = split(a)
    bh, bl = split(b)
    dot = functools.partial(
        lax.dot_general, dimension_numbers=(dims, ((), ())), preferred_element_type=jnp.float32
    )
    return dot(ah, bh) + (dot(ah, bl) + dot(al, bh))


def nt(a, b):
    return three(a, b, ((1,), (1,)))


def nn(a, b):
    return three(a, b, ((1,), (0,)))


def tn(a, b):
    return three(a, b, ((0,), (0,)))


def total(terms):
    while len(terms) > 1:
        terms = [
            terms[i] + terms[i + 1] if i + 1 < len(terms) else terms[i]
            for i in range(0, len(terms), 2)
        ]
    return terms[0]


def spread_lane(block, lane):
    return jnp.broadcast_to(block[:, lane : lane + 1], (S, B))


def pick_lane(block, lane):
    return jnp.take_along_axis(block, jnp.full((S, B), lane, jnp.int32), axis=1)


def spread_row(block, row):
    return jnp.broadcast_to(block[row : row + 1, :], (S, B))


def base_factor(tile_ref, upper_ref, inv_ref):
    groups = B // S
    sub = lax.broadcasted_iota(jnp.int32, (S, B), 0)
    lane = lax.broadcasted_iota(jnp.int32, (S, B), 1)
    left = [tile_ref[S * g : S * g + S, :] for g in range(groups)]
    for b in range(groups):
        a = left[b]
        q = jnp.where(lane < S * b, a, jnp.where(lane == sub + S * b, 1.0, 0.0))
        cols = [pick_lane(a, S * b + j) for j in range(S)]
        e = [[spread_row(cols[j], i) if j <= i else None for j in range(S)] for i in range(S)]
        inv, low = [], [[None] * S for _ in range(S)]
        for j in range(S):
            inv.append(1.0 / e[j][j])
            for i in range(j + 1, S):
                low[i][j] = e[i][j] * inv[j]
            for k in range(j + 1, S):
                for i in range(k, S):
                    e[i][k] = e[i][k] - low[i][j] * e[k][j]
        ra = [spread_row(a, i) for i in range(S)]
        rq = [spread_row(q, i) for i in range(S)]
        for j in range(S):
            for i in range(j + 1, S):
                ra[i] = ra[i] - low[i][j] * ra[j]
                rq[i] = rq[i] - low[i][j] * rq[j]
        xa, xq = None, None
        for j in range(S):
            root = lax.rsqrt(e[j][j])
            ya, yq = ra[j] * root, rq[j] * root
            xa = ya if xa is None else jnp.where(sub == j, ya, xa)
            xq = yq if xq is None else jnp.where(sub == j, yq, xq)
        upper_ref[S * b : S * b + S, :] = jnp.where(lane >= sub + S * b, xa, 0.0)
        inv_ref[S * b : S * b + S, :] = xq
        if b + 1 == groups:
            break
        done = lane < S * b + S
        w = [jnp.where(done, rq[j], ra[j]) * inv[j] for j in range(S)]
        for i in range(S - 1, 0, -1):
            for j in range(i):
                w[j] = w[j] - low[i][j] * w[i]
        pivots = done & (lane >= S * b)
        for g in range(b + 1, min(b + 1 + NEAR, groups)):
            m = [spread_lane(left[g], S * b + j) for j in range(S)]
            left[g] = jnp.where(pivots, 0.0, left[g]) - total([m[j] * w[j] for j in range(S)])
        far = b + 1 + NEAR
        if far < groups:
            packed = w[0]
            for j in range(1, S):
                packed = jnp.where(sub == j, w[j], packed)
            rows = [packed if g == b else jnp.zeros((S, B), jnp.float32) for g in range(groups)]
            moved = nn(jnp.concatenate(left[far:], axis=0), jnp.concatenate(rows, axis=0))
            for g in range(far, groups):
                at = S * (g - far)
                left[g] = jnp.where(pivots, 0.0, left[g]) - moved[at : at + S, :]


def panel_kernel(
    tiles, layers, diag_ref, basis_ref, ranks_ref, cores_ref,
    factor_ref, z_ref, diag_out, cores_out,
    work, low, block, upper, inverse, masked_t, col, oth, w_rows, w_cols, gram,
    local, recv_work, send_work, recv_low, send_low, recv_z, send_z,
    recvc, sendc, recvo, sendo,
):
    t = lax.axis_index("tile")
    l = lax.axis_index("layer")
    rows, order = diag_ref.shape[1], diag_ref.shape[2]
    rmax = basis_ref.shape[0]
    panels = order // B
    early = order - B
    span = cores_ref.shape[1]
    half = tiles // 2
    hub = (t == 0) & (l == 0)
    spoke = jnp.logical_not(hub)
    fan = ((t == 0) & (l > 0)) | ((t == 1) & (l == 0))
    side = (t % 2 == 0) & spoke

    def remote(src, dst, send, recv, to_t, to_l):
        return pltpu.make_async_remote_copy(
            src_ref=src, dst_ref=dst, send_sem=send, recv_sem=recv,
            device_id=(to_t, to_l), device_id_type=pl.DeviceIdType.MESH,
        )

    def each(count, act):
        lax.fori_loop(0, count, lambda i, c: (act(i), c)[1], 0)

    def needed(j, piece):
        return (piece + 1) * rows > j * B

    def columns(j):
        return pl.ds(pl.multiple_of(j * B, B), B)

    def slot(j, piece):
        return work.at[j, pl.ds(pl.multiple_of(piece * rows, S), rows), :]

    def gathered(j):
        return remote(
            diag_ref.at[0, :, columns(j)], slot(j, l), send_work.at[j], recv_work.at[j, l], 0, 0
        )

    def kept(j):
        return pltpu.make_async_copy(
            diag_ref.at[0, :, columns(j)], slot(j, 0), recv_work.at[j, 0]
        )

    def landed(j, piece):
        return remote(slot(j, piece), slot(j, piece), send_work.at[j], recv_work.at[j, piece], t, l)

    def parts(k):
        whole, cut = (k * B) // rows, (k * B) % rows
        if cut:
            return [(l == whole, whole, whole + 1, cut), (l > whole, whole + 1, layers, 0)]
        return [(l >= whole, whole, layers, 0)]

    def down_low(k, at, to_t, child):
        piece = factor_ref.at[0, at:, k * B : k * B + B]
        return remote(piece, piece, send_low.at[k, child], recv_low.at[k], to_t, l)

    def out_low(k, at, piece):
        return remote(
            low.at[pl.ds(pl.multiple_of(piece * rows + at, S), rows - at), k * B : k * B + B],
            factor_ref.at[0, at:, k * B : k * B + B],
            send_low.at[k, piece], recv_low.at[k], jnp.where(piece == 0, 1, 0), piece,
        )

    def out_z(part, piece):
        cut = z_ref.at[:, early:] if part else z_ref.at[:, :early]
        return remote(
            cut, cut, send_z.at[part, piece], recv_z.at[part], jnp.where(piece == 0, 1, 0), piece
        )

    def down_z(part, to_t, child):
        cut = z_ref.at[:, early:] if part else z_ref.at[:, :early]
        return remote(cut, cut, send_z.at[part, child], recv_z.at[part], to_t, l)

    def onward(copy, act):
        @pl.when(fan)
        def _():
            each(half - 1, lambda i: act(copy(2 * (half - 1 - i), half - 1 - i)))

        @pl.when(side)
        def _():
            act(copy(t + 1, 0))

    def start(copy):
        copy.start()

    def sent(copy):
        copy.wait_send()

    def column_to(to_l):
        return remote(cores_ref.at[0, 0], col, sendc.at[to_l], recvc, t, to_l)

    def column_kept():
        return pltpu.make_async_copy(cores_ref.at[0, 0], col, recvc)

    def other_to(to_t):
        return remote(
            cores_ref.at[0, 0], oth.at[t % span], sendo.at[to_t], recvo.at[t % span], to_t, t // span
        )

    def other_kept():
        return pltpu.make_async_copy(cores_ref.at[0, 0], oth.at[t % span], recvo.at[t % span])

    basis_in = pltpu.make_async_copy(basis_ref, masked_t, local.at[0])
    diag_in = pltpu.make_async_copy(diag_ref, diag_out, local.at[1])
    cores_in = pltpu.make_async_copy(cores_ref, cores_out, local.at[2])

    def mask():
        basis_in.wait()
        row = lax.broadcasted_iota(jnp.int32, (rmax, order), 0)
        masked_t[...] = masked_t[...] * jnp.where(row < ranks_ref[0], 1.0, 0.0)

    barrier = pltpu.get_barrier_semaphore()
    devices = tiles * layers

    @pl.when(hub)
    def _():
        each(panels, lambda j: pl.when(needed(j, 0))(lambda: kept(j).start()))
        basis_in.start()

        def greet(i):
            pl.semaphore_signal(
                barrier, inc=1, device_id=((i + 1) // layers, (i + 1) % layers),
                device_id_type=pl.DeviceIdType.MESH,
            )

        each(devices - 1, greet)

    @pl.when(spoke)
    def _():
        factor_ref[...] = jnp.zeros_like(factor_ref)
        pl.semaphore_signal(barrier, inc=1, device_id=(0, 0), device_id_type=pl.DeviceIdType.MESH)
        pl.semaphore_wait(barrier, 1)

    def gather(j):
        if 0 < j <= panels:
            pl.when((t == 0) & spoke & needed(j - 1, l))(lambda: gathered(j - 1).wait_send())
        if j < panels:
            pl.when((t == 0) & spoke & needed(j, l))(lambda: gathered(j).start())

    for j in range(3):
        gather(j)

    diag_in.start()
    cores_in.start()

    @pl.when(hub)
    def _():
        low[...] = jnp.zeros_like(low)

        def panel(k, carry):
            at = pl.ds(pl.multiple_of(k * B, B), B)

            @pl.when(needed(k, 0))
            def _():
                kept(k).wait()

            def take(piece):
                pl.when(needed(k, piece + 1))(lambda: landed(k, piece + 1).wait_recv())

            each(layers - 1, take)

            for c in range(panels):
                @pl.when(k == c)
                def _():
                    here = slice(c * B, c * B + B)
                    if c:
                        work2 = work[c, c * B :, :] - nt(low[c * B :, : c * B], low[here, : c * B])
                        low[c * B :, here] = work2
                    else:
                        low[:, here] = work[0]
            block[...] = low[at, at]

            base_factor(block, upper, inverse)
            low[at, at] = upper[...].T

            @pl.when(k == 0)
            def _():
                mask()
                pl.semaphore_wait(barrier, devices - 1)

            for c in range(panels):
                @pl.when(k == c)
                def _():
                    here = slice(c * B, c * B + B)
                    rest = slice(c * B + B, order)
                    if c + 1 < panels:
                        low[rest, here] = nt(low[rest, here], inverse[...])
                    part = masked_t[:, here]
                    if c:
                        part = part - nt(z_ref[:, : c * B], low[here, : c * B])
                    z_ref[:, here] = nt(part, inverse[...])
                    if c == panels - 1:
                        each(layers, lambda piece: out_z(1, piece).start())
                    for _, first, last, cut in parts(c):
                        each(last - first, lambda i: out_low(c, cut, first + i).start())
                    if c == panels - 2:
                        each(layers, lambda piece: out_z(0, piece).start())
            return carry

        lax.fori_loop(0, panels, panel, 0)
        factor_ref[0] = low[:rows, :]

    @pl.when(spoke)
    def _():
        basis_in.start()

        def relay(k):
            for mine, _, _, cut in parts(k):
                @pl.when(mine)
                def _():
                    down_low(k, cut, t, 0).wait_recv()
                    onward(lambda to_t, child: down_low(k, cut, to_t, child), start)

            gather(k + 3)

        relay(0)

        @pl.when(t > 0)
        def _():
            @pl.when(l == 0)
            def _():
                each(layers - 1, lambda i: column_to(i + 1).start())
                column_kept().start()

                def other(i):
                    to_t = 1 + lax.rem(t - 1 + i, tiles - 1)
                    pl.when((to_t != t) | (t // span != 0))(lambda: other_to(to_t).start())

                each(tiles - 1, other)
                pl.when(t // span == 0)(lambda: other_kept().start())

        relay(1)

        @pl.when(t > 0)
        def _():
            pl.when(l == 0)(lambda: column_kept().wait())
            pl.when(l != 0)(lambda: column_to(0).wait_recv())

            def take_other(s):
                mine = (l == 0) & (l * span + s == t)

                @pl.when(mine)
                def _():
                    pltpu.make_async_copy(cores_ref.at[0, 0], oth.at[s], recvo.at[s]).wait()

                @pl.when(jnp.logical_not(mine) & (l * span + s > 0))
                def _():
                    remote(cores_ref.at[0, 0], oth.at[s], sendo.at[0], recvo.at[s], t, l).wait_recv()

            each(span, take_other)
            mask()
            w_cols[...] = tn(col[...], masked_t[...])
            own = masked_t[...].T
            w_rows[...] = nn(own, col[...])

        for k in range(2, panels - 1):
            relay(k)
        down_z(0, t, 0).wait_recv()
        onward(lambda to_t, child: down_z(0, to_t, child), start)
        gram[...] = nt(z_ref[:, :early], z_ref[:, :early])
        down_z(1, t, 0).wait_recv()
        onward(lambda to_t, child: down_z(1, to_t, child), start)
        relay(panels - 1)

        @pl.when(t == 0)
        def _():
            basis_in.wait()

    diag_in.wait()
    cores_in.wait()

    @pl.when(t > 0)
    def _():
        mine = pl.ds(pl.multiple_of(l * rows, S), rows)
        square = gram[...] + nt(z_ref[:, early:], z_ref[:, early:])
        partial = nn(w_rows[mine, :], square)
        diag_out[0] = diag_out[0] - nn(partial, w_cols[...])
        coef = nn(col[...], square)
        for s in range(span):
            other_id = l * span + s

            @pl.when((t > other_id) & (other_id > 0))
            def _():
                cores_out[0, s] = cores_out[0, s] - nt(coef, oth[s])

    @pl.when(hub)
    def _():
        for c in range(panels):
            for _, first, last, cut in parts(c):
                each(last - first, lambda i: out_low(c, cut, first + i).wait_send())
        for part in range(2):
            each(layers, lambda piece: out_z(part, piece).wait_send())

    @pl.when(spoke)
    def _():
        for k in range(panels):
            for mine, _, _, cut in parts(k):
                @pl.when(mine)
                def _():
                    onward(lambda to_t, child: down_low(k, cut, to_t, child), sent)
        for part in range(2):
            onward(lambda to_t, child: down_z(part, to_t, child), sent)

    @pl.when((l == 0) & (t > 0))
    def _():
        each(layers - 1, lambda i: column_to(i + 1).wait_send())

        def other(i):
            to_t = 1 + lax.rem(t - 1 + i, tiles - 1)
            pl.when((to_t != t) | (t // span != 0))(lambda: other_to(to_t).wait_send())

        each(tiles - 1, other)


def emit_kernel(a, b, c, d, a_out, b_out, c_out, d_out, sems):
    copies = [
        pltpu.make_async_copy(src, dst, sems.at[i])
        for i, (src, dst) in enumerate(((a, a_out), (c, c_out), (b, b_out), (d, d_out)))
    ]
    for copy in copies:
        copy.start()
    for copy in copies:
        copy.wait()


def fixed(x):
    return pltpu.with_memory_space_constraint(x, pltpu.HBM)


def body(tiles, layers, basis, ranks, cores, diag):
    rmax = basis.shape[2]
    span = cores.shape[1]
    rows, order = diag.shape[1], diag.shape[2]
    panels = order // B
    vm = pl.BlockSpec(memory_space=pltpu.VMEM)
    hbm = pl.BlockSpec(memory_space=pl.ANY)
    f32 = jnp.float32
    dma = pltpu.SemaphoreType.DMA
    shapes = ((1, rows, order), (rmax, order), diag.shape, cores.shape)
    children = max(layers, tiles // 2)
    results = pl.pallas_call(
        functools.partial(panel_kernel, tiles, layers),
        out_shape=tuple(pltpu.VMEM(shape, f32) for shape in shapes),
        in_specs=[hbm, hbm, pl.BlockSpec(memory_space=pltpu.SMEM), hbm],
        out_specs=(vm,) * 4,
        scratch_shapes=[
            pltpu.VMEM((panels, order, B), f32),
            pltpu.VMEM((order, order), f32),
            pltpu.VMEM((B, B), f32),
            pltpu.VMEM((B, B), f32),
            pltpu.VMEM((B, B), f32),
            pltpu.VMEM((rmax, order), f32),
            pltpu.VMEM((rmax, rmax), f32),
            pltpu.VMEM((span, rmax, rmax), f32),
            pltpu.VMEM((order, rmax), f32),
            pltpu.VMEM((rmax, order), f32),
            pltpu.VMEM((rmax, rmax), f32),
            dma((3,)),
            dma((panels, layers)),
            dma((panels,)),
            dma((panels,)),
            dma((panels, children)),
            dma((2,)),
            dma((2, children)),
            dma,
            dma((layers,)),
            dma((span,)),
            dma((tiles,)),
        ],
        compiler_params=pltpu.CompilerParams(
            collective_id=0, has_side_effects=True, vmem_limit_bytes=24 << 20
        ),
    )(fixed(diag), fixed(basis[0].T), ranks, fixed(cores))
    factors, zt, schur, couplings = pl.pallas_call(
        emit_kernel,
        out_shape=tuple(jax.ShapeDtypeStruct(shape, f32) for shape in shapes),
        in_specs=[vm] * 4,
        out_specs=(hbm,) * 4,
        scratch_shapes=[dma((4,))],
        compiler_params=pltpu.CompilerParams(vmem_limit_bytes=1 << 20),
    )(*results)
    return factors, zt.T[None], schur, couplings


def solution(mesh):
    placed = (
        P("tile", None, None),
        P("tile"),
        P("tile", "layer", None, None),
        P("tile", "layer", None),
    )
    return jax.shard_map(
        functools.partial(body, mesh.shape["tile"], mesh.shape["layer"]),
        mesh=mesh,
        in_specs=placed,
        out_specs=(
            P(None, "layer", None),
            P(),
            P("tile", "layer", None),
            P("tile", "layer", None, None),
        ),
        check_vma=False,
    )
```

```python
import functools

import jax
import jax.numpy as jnp
from jax import lax
from jax.experimental import pallas as pl
from jax.experimental.pallas import tpu as pltpu
from jax.sharding import PartitionSpec as P

B = 128
S = 8
NEAR = 2


def split(a):
    high = a.astype(jnp.bfloat16)
    return high, (a - high.astype(jnp.float32)).astype(jnp.bfloat16)


def three(a, b, dims):
    ah, al = split(a)
    bh, bl = split(b)
    dot = functools.partial(
        lax.dot_general, dimension_numbers=(dims, ((), ())), preferred_element_type=jnp.float32
    )
    return dot(ah, bh) + (dot(ah, bl) + dot(al, bh))


def nt(a, b):
    return three(a, b, ((1,), (1,)))


def nn(a, b):
    return three(a, b, ((1,), (0,)))


def tn(a, b):
    return three(a, b, ((0,), (0,)))


def pair_nt(a, b):
    (ah, al), (bh, bl) = a, b
    dot = functools.partial(
        lax.dot_general, dimension_numbers=(((1,), (1,)), ((), ())), preferred_element_type=jnp.float32
    )
    return dot(ah, bh) + dot(jnp.concatenate([ah, al], axis=1), jnp.concatenate([bl, bh], axis=1))


def total(terms):
    while len(terms) > 1:
        terms = [
            terms[i] + terms[i + 1] if i + 1 < len(terms) else terms[i]
            for i in range(0, len(terms), 2)
        ]
    return terms[0]


def spread_lane(block, lane):
    return jnp.broadcast_to(block[:, lane : lane + 1], (S, B))


def pick_lane(block, lane):
    return jnp.take_along_axis(block, jnp.full((S, B), lane, jnp.int32), axis=1)


def spread_row(block, row):
    return jnp.broadcast_to(block[row : row + 1, :], (S, B))


def base_factor(tile_ref, upper_ref, inv_ref):
    groups = B // S
    sub = lax.broadcasted_iota(jnp.int32, (S, B), 0)
    lane = lax.broadcasted_iota(jnp.int32, (S, B), 1)
    left = [tile_ref[S * g : S * g + S, :] for g in range(groups)]
    for b in range(groups):
        a = left[b]
        q = jnp.where(lane < S * b, a, jnp.where(lane == sub + S * b, 1.0, 0.0))
        cols = [pick_lane(a, S * b + j) for j in range(S)]
        e = [[spread_row(cols[j], i) if j <= i else None for j in range(S)] for i in range(S)]
        inv, low = [], [[None] * S for _ in range(S)]
        for j in range(S):
            inv.append(1.0 / e[j][j])
            for i in range(j + 1, S):
                low[i][j] = e[i][j] * inv[j]
            for k in range(j + 1, S):
                for i in range(k, S):
                    e[i][k] = e[i][k] - low[i][j] * e[k][j]
        ra = [spread_row(a, i) for i in range(S)]
        rq = [spread_row(q, i) for i in range(S)]
        for j in range(S):
            for i in range(j + 1, S):
                ra[i] = ra[i] - low[i][j] * ra[j]
                rq[i] = rq[i] - low[i][j] * rq[j]
        xa, xq = None, None
        for j in range(S):
            root = lax.rsqrt(e[j][j])
            ya, yq = ra[j] * root, rq[j] * root
            xa = ya if xa is None else jnp.where(sub == j, ya, xa)
            xq = yq if xq is None else jnp.where(sub == j, yq, xq)
        upper_ref[S * b : S * b + S, :] = jnp.where(lane >= sub + S * b, xa, 0.0)
        inv_ref[S * b : S * b + S, :] = xq
        if b + 1 == groups:
            break
        done = lane < S * b + S
        w = [jnp.where(done, rq[j], ra[j]) * inv[j] for j in range(S)]
        for i in range(S - 1, 0, -1):
            for j in range(i):
                w[j] = w[j] - low[i][j] * w[i]
        pivots = done & (lane >= S * b)
        for g in range(b + 1, min(b + 1 + NEAR, groups)):
            m = [spread_lane(left[g], S * b + j) for j in range(S)]
            left[g] = jnp.where(pivots, 0.0, left[g]) - total([m[j] * w[j] for j in range(S)])
        far = b + 1 + NEAR
        if far < groups:
            packed = w[0]
            for j in range(1, S):
                packed = jnp.where(sub == j, w[j], packed)
            rows = [packed if g == b else jnp.zeros((S, B), jnp.float32) for g in range(groups)]
            moved = nn(jnp.concatenate(left[far:], axis=0), jnp.concatenate(rows, axis=0))
            for g in range(far, groups):
                at = S * (g - far)
                left[g] = jnp.where(pivots, 0.0, left[g]) - moved[at : at + S, :]


def panel_kernel(
    tiles, layers, diag_ref, basis_ref, ranks_ref, cores_ref,
    factor_ref, z_ref, diag_out, cores_out,
    work, low, low_h, low_l, inv_h, inv_l, z_h, z_l, z_rest, corr, block, upper, inverse, masked_t, col, oth, w_rows, w_cols, gram,
    local, recv_work, send_work, recv_low, send_low, recv_z, send_z,
    recvc, sendc, recvo, sendo,
):
    t = lax.axis_index("tile")
    l = lax.axis_index("layer")
    rows, order = diag_ref.shape[1], diag_ref.shape[2]
    rmax = basis_ref.shape[0]
    panels = order // B
    early = order - B
    span = cores_ref.shape[1]
    half = tiles // 2
    hub = (t == 0) & (l == 0)
    spoke = jnp.logical_not(hub)
    fan = ((t == 0) & (l > 0)) | ((t == 1) & (l == 0))
    side = (t % 2 == 0) & spoke

    def remote(src, dst, send, recv, to_t, to_l):
        return pltpu.make_async_remote_copy(
            src_ref=src, dst_ref=dst, send_sem=send, recv_sem=recv,
            device_id=(to_t, to_l), device_id_type=pl.DeviceIdType.MESH,
        )

    def each(count, act):
        lax.fori_loop(0, count, lambda i, c: (act(i), c)[1], 0)

    def needed(j, piece):
        return (piece + 1) * rows > j * B

    def parcels(piece):
        top, end = piece * rows, (piece + 1) * rows
        wide = min(2 * B, order)
        cuts = [(0, B, 0, B), (B, 2 * B, 0, wide), (2 * B, 3 * B, 0, wide), (3 * B, order, 0, wide)]
        cuts += [(j * B, order, j * B, j * B + B) for j in range(2, panels)]
        found = []
        for tag, (r0, r1, c0, c1) in enumerate(cuts):
            r0, r1 = max(r0, top), min(r1, end)
            if r0 < r1:
                found.append((tag, r0, r1, c0, c1))
        return found

    def gathered(piece, tag, r0, r1, c0, c1):
        return remote(
            diag_ref.at[0, r0 - piece * rows : r1 - piece * rows, c0:c1], work.at[r0:r1, c0:c1],
            send_work.at[tag], recv_work.at[piece, tag], 0, 0,
        )

    def kept(tag, r0, r1, c0, c1):
        return pltpu.make_async_copy(
            diag_ref.at[0, r0:r1, c0:c1], work.at[r0:r1, c0:c1], recv_work.at[0, tag]
        )

    def parts(k):
        whole, cut = (k * B) // rows, (k * B) % rows
        if cut:
            return [(l == whole, whole, whole + 1, cut), (l > whole, whole + 1, layers, 0)]
        return [(l >= whole, whole, layers, 0)]

    def down_low(k, at, to_t, child):
        piece = factor_ref.at[0, at:, k * B : k * B + B]
        return remote(piece, piece, send_low.at[k, child], recv_low.at[k], to_t, l)

    def out_low(k, at, piece):
        return remote(
            low.at[pl.ds(pl.multiple_of(piece * rows + at, S), rows - at), k * B : k * B + B],
            factor_ref.at[0, at:, k * B : k * B + B],
            send_low.at[k, piece], recv_low.at[k], jnp.where(piece == 0, 1, 0), piece,
        )

    edges = (0, panels // 2 * B, early, order)

    def z_part(part):
        return z_ref.at[:, edges[part] : edges[part + 1]]

    def out_z(part, piece):
        return remote(
            z_part(part), z_part(part), send_z.at[part, piece], recv_z.at[part],
            jnp.where(piece == 0, 1, 0), piece,
        )

    def down_z(part, to_t, child):
        return remote(z_part(part), z_part(part), send_z.at[part, child], recv_z.at[part], to_t, l)

    def onward(copy, act):
        @pl.when(fan)
        def _():
            each(half - 1, lambda i: act(copy(2 * (half - 1 - i), half - 1 - i)))

        @pl.when(side)
        def _():
            act(copy(t + 1, 0))

    def start(copy):
        copy.start()

    def sent(copy):
        copy.wait_send()

    def column_to(to_l):
        return remote(cores_ref.at[0, 0], col, sendc.at[to_l], recvc, t, to_l)

    def column_kept():
        return pltpu.make_async_copy(cores_ref.at[0, 0], col, recvc)

    def other_to(to_t):
        return remote(
            cores_ref.at[0, 0], oth.at[t % span], sendo.at[to_t], recvo.at[t % span], to_t, t // span
        )

    def other_kept():
        return pltpu.make_async_copy(cores_ref.at[0, 0], oth.at[t % span], recvo.at[t % span])

    basis_in = pltpu.make_async_copy(basis_ref, masked_t, local.at[0])
    diag_in = pltpu.make_async_copy(diag_ref, diag_out, local.at[1])
    cores_in = pltpu.make_async_copy(cores_ref, cores_out, local.at[2])

    def mask():
        basis_in.wait()
        row = lax.broadcasted_iota(jnp.int32, (rmax, order), 0)
        masked_t[...] = masked_t[...] * jnp.where(row < ranks_ref[0], 1.0, 0.0)

    barrier = pltpu.get_barrier_semaphore()
    devices = tiles * layers

    @pl.when(hub)
    def _():
        for parcel in parcels(0):
            kept(*parcel).start()
        basis_in.start()

        def greet(i):
            pl.semaphore_signal(
                barrier, inc=1, device_id=((i + 1) // layers, (i + 1) % layers),
                device_id_type=pl.DeviceIdType.MESH,
            )

        each(devices - 1, greet)

    @pl.when(spoke)
    def _():
        factor_ref[...] = jnp.zeros_like(factor_ref)
        pl.semaphore_signal(barrier, inc=1, device_id=(0, 0), device_id_type=pl.DeviceIdType.MESH)
        pl.semaphore_wait(barrier, 1)

    def gather(step):
        for piece in range(1, layers):
            moves = parcels(piece)
            now = [(m, True) for m in moves[step : step + 1]]
            if step > 1:
                now = [(m, False) for m in moves[step - 2 : step - 1]] + now
            if now:
                @pl.when((t == 0) & (l == piece))
                def _():
                    for move, begin in now:
                        copy = gathered(piece, *move)
                        copy.start() if begin else copy.wait_send()

    for step in range(4):
        gather(step)

    diag_in.start()
    cores_in.start()

    def land(piece, parcel):
        if piece:
            gathered(piece, *parcel).wait_recv()
        else:
            kept(*parcel).wait()

    def arrived(tag, block_row=None):
        for piece in range(layers):
            for parcel in parcels(piece):
                if parcel[0] != tag:
                    continue
                near = block_row is None or (
                    piece * rows < (block_row + 1) * B and (piece + 1) * rows > block_row * B
                )
                yield near, functools.partial(land, piece, parcel)

    def await_near(tag, block_row):
        for near, wait in arrived(tag, block_row):
            if near:
                wait()

    def await_far(tag, block_row):
        for near, wait in arrived(tag, block_row):
            if not near:
                wait()

    def await_all(tag):
        for _, wait in arrived(tag):
            wait()

    def span_of(first, last):
        return slice(first * B, last * B)

    def halves(r, c):
        return low_h[r, c], low_l[r, c]

    def put(r, c, value):
        low[r, c] = value
        low_h[r, c], low_l[r, c] = split(value)

    def inverse_of(k):
        return inv_h[k], inv_l[k]

    def catch_up(k, first, last):
        r = span_of(first, last)
        done, here = span_of(k - 1, k), span_of(k, k + 1)
        put(r, done, pair_nt(split(work[r, done]), inverse_of(k - 1)))
        before = span_of(0, k)
        work[r, here] = work[r, here] - pair_nt(halves(r, before), halves(here, before))

    def stage(k):
        here, following = span_of(k, k + 1), span_of(k + 1, k + 2)
        if k:
            before = span_of(0, k)
            z_rest[...] = masked_t[:, here] - pair_nt(
                (z_h[:, before], z_l[:, before]), halves(here, before)
            )
            if k + 1 < panels:
                catch_up(k, k + 1, k + 2 if k == 1 else panels)
                corr[...] = pair_nt(halves(following, before), halves(following, before))
        base_factor(block, upper, inverse)

    def settle(k):
        here, following = span_of(k, k + 1), span_of(k + 1, k + 2)
        inv = split(inverse[...])
        inv_h[k], inv_l[k] = inv
        put(here, here, upper[...].T)
        if k + 1 < panels:
            below = pair_nt(split(work[following, here]), inv)
            put(following, here, below)
            parts_of = split(below)
            rest = work[following, following] - pair_nt(parts_of, parts_of)
            block[...] = rest - corr[...] if k else rest
        part = z_rest[...] if k else masked_t[:, here]
        solved = pair_nt(split(part), inv)
        z_ref[:, here] = solved
        z_h[:, here], z_l[:, here] = split(solved)

    def ship_low(c):
        for _, first, last, cut in parts(c):
            for piece in range(first, last):
                out_low(c, cut, piece).start()

    def ship_z(part):
        for piece in range(layers):
            out_z(part, piece).start()

    @pl.when(hub)
    def _():
        await_all(0)
        block[...] = work[:B, :B]
        for k in range(panels):
            if k == 1:
                await_all(2)
            if k > 1:
                await_far(k + 2, k)
            stage(k)
            if k == 0:
                mask()
                await_all(1)
            elif k + 1 < panels:
                await_near(k + 3, k + 1)
            settle(k)
            if k == 1:
                await_all(3)
                catch_up(1, 3, panels)
                pl.semaphore_wait(barrier, devices - 1)
            if k == panels - 1:
                ship_z(2)
                ship_low(k)
            elif k:
                ship_low(k - 1)
            if k == panels - 2:
                ship_low(k)
                ship_z(1)
            if k == panels // 2 - 1:
                ship_z(0)
        factor_ref[...] = jnp.zeros_like(factor_ref)
        for c in range(panels):
            r0, r1 = c * B, min(rows, order)
            if r0 < r1:
                factor_ref[0, r0:r1, c * B : c * B + B] = low[r0:r1, c * B : c * B + B]

    @pl.when(spoke)
    def _():
        basis_in.start()

        def relay(k):
            for mine, _, _, cut in parts(k):
                @pl.when(mine)
                def _():
                    down_low(k, cut, t, 0).wait_recv()
                    onward(lambda to_t, child: down_low(k, cut, to_t, child), start)

            gather(k + 4)

        relay(0)

        @pl.when(t > 0)
        def _():
            @pl.when(l == 0)
            def _():
                each(layers - 1, lambda i: column_to(i + 1).start())
                column_kept().start()

                def other(i):
                    to_t = 1 + lax.rem(t - 1 + i, tiles - 1)
                    pl.when((to_t != t) | (t // span != 0))(lambda: other_to(to_t).start())

                each(tiles - 1, other)
                pl.when(t // span == 0)(lambda: other_kept().start())

        relay(1)

        @pl.when(t > 0)
        def _():
            pl.when(l == 0)(lambda: column_kept().wait())
            pl.when(l != 0)(lambda: column_to(0).wait_recv())

            def take_other(s):
                mine = (l == 0) & (l * span + s == t)

                @pl.when(mine)
                def _():
                    pltpu.make_async_copy(cores_ref.at[0, 0], oth.at[s], recvo.at[s]).wait()

                @pl.when(jnp.logical_not(mine) & (l * span + s > 0))
                def _():
                    remote(cores_ref.at[0, 0], oth.at[s], sendo.at[0], recvo.at[s], t, l).wait_recv()

            each(span, take_other)
            mask()
            w_cols[...] = tn(col[...], masked_t[...])
            own = masked_t[...].T
            w_rows[...] = nn(own, col[...])

        def relay_z(part):
            down_z(part, t, 0).wait_recv()
            onward(lambda to_t, child: down_z(part, to_t, child), start)

        for k in range(2, panels - 1):
            if k == panels // 2 - 1:
                relay_z(0)
            relay(k)
        relay_z(1)
        gram[...] = nt(z_ref[:, :early], z_ref[:, :early])
        relay_z(2)
        relay(panels - 1)

        for step in range(panels + 4, panels + 8):
            gather(step)

        @pl.when(t == 0)
        def _():
            basis_in.wait()

    diag_in.wait()
    cores_in.wait()

    @pl.when(t > 0)
    def _():
        mine = pl.ds(pl.multiple_of(l * rows, S), rows)
        square = gram[...] + nt(z_ref[:, early:], z_ref[:, early:])
        partial = nn(w_rows[mine, :], square)
        diag_out[0] = diag_out[0] - nn(partial, w_cols[...])
        coef = nn(col[...], square)
        for s in range(span):
            other_id = l * span + s

            @pl.when((t > other_id) & (other_id > 0))
            def _():
                cores_out[0, s] = cores_out[0, s] - nt(coef, oth[s])

    @pl.when(hub)
    def _():
        for c in range(panels):
            for _, first, last, cut in parts(c):
                each(last - first, lambda i: out_low(c, cut, first + i).wait_send())
        for part in range(3):
            each(layers, lambda piece: out_z(part, piece).wait_send())

    @pl.when(spoke)
    def _():
        for k in range(panels):
            for mine, _, _, cut in parts(k):
                @pl.when(mine)
                def _():
                    onward(lambda to_t, child: down_low(k, cut, to_t, child), sent)
        for part in range(3):
            onward(lambda to_t, child: down_z(part, to_t, child), sent)

    @pl.when((l == 0) & (t > 0))
    def _():
        each(layers - 1, lambda i: column_to(i + 1).wait_send())

        def other(i):
            to_t = 1 + lax.rem(t - 1 + i, tiles - 1)
            pl.when((to_t != t) | (t // span != 0))(lambda: other_to(to_t).wait_send())

        each(tiles - 1, other)


def emit_kernel(a, b, c, d, a_out, b_out, c_out, d_out, sems):
    copies = [
        pltpu.make_async_copy(src, dst, sems.at[i])
        for i, (src, dst) in enumerate(((a, a_out), (c, c_out), (b, b_out), (d, d_out)))
    ]
    for copy in copies:
        copy.start()
    for copy in copies:
        copy.wait()


def fixed(x):
    return pltpu.with_memory_space_constraint(x, pltpu.HBM)


def body(tiles, layers, basis, ranks, cores, diag):
    rmax = basis.shape[2]
    span = cores.shape[1]
    rows, order = diag.shape[1], diag.shape[2]
    panels = order // B
    vm = pl.BlockSpec(memory_space=pltpu.VMEM)
    hbm = pl.BlockSpec(memory_space=pl.ANY)
    f32, bf16 = jnp.float32, jnp.bfloat16
    dma = pltpu.SemaphoreType.DMA
    shapes = ((1, rows, order), (rmax, order), diag.shape, cores.shape)
    children = max(layers, tiles // 2)
    results = pl.pallas_call(
        functools.partial(panel_kernel, tiles, layers),
        out_shape=tuple(pltpu.VMEM(shape, f32) for shape in shapes),
        in_specs=[hbm, hbm, pl.BlockSpec(memory_space=pltpu.SMEM), hbm],
        out_specs=(vm,) * 4,
        scratch_shapes=[
            pltpu.VMEM((order, order), f32),
            pltpu.VMEM((order, order), f32),
            pltpu.VMEM((order, order), bf16),
            pltpu.VMEM((order, order), bf16),
            pltpu.VMEM((panels, B, B), bf16),
            pltpu.VMEM((panels, B, B), bf16),
            pltpu.VMEM((rmax, order), bf16),
            pltpu.VMEM((rmax, order), bf16),
            pltpu.VMEM((rmax, B), f32),
            pltpu.VMEM((B, B), f32),
            pltpu.VMEM((B, B), f32),
            pltpu.VMEM((B, B), f32),
            pltpu.VMEM((B, B), f32),
            pltpu.VMEM((rmax, order), f32),
            pltpu.VMEM((rmax, rmax), f32),
            pltpu.VMEM((span, rmax, rmax), f32),
            pltpu.VMEM((order, rmax), f32),
            pltpu.VMEM((rmax, order), f32),
            pltpu.VMEM((rmax, rmax), f32),
            dma((3,)),
            dma((layers, panels + 2)),
            dma((panels + 2,)),
            dma((panels,)),
            dma((panels, children)),
            dma((3,)),
            dma((3, children)),
            dma,
            dma((layers,)),
            dma((span,)),
            dma((tiles,)),
        ],
        compiler_params=pltpu.CompilerParams(
            collective_id=0, has_side_effects=True, vmem_limit_bytes=24 << 20
        ),
    )(fixed(diag), fixed(basis[0].T), ranks, fixed(cores))
    factors, zt, schur, couplings = pl.pallas_call(
        emit_kernel,
        out_shape=tuple(jax.ShapeDtypeStruct(shape, f32) for shape in shapes),
        in_specs=[vm] * 4,
        out_specs=(hbm,) * 4,
        scratch_shapes=[dma((4,))],
        compiler_params=pltpu.CompilerParams(vmem_limit_bytes=1 << 20),
    )(*results)
    return factors, zt.T[None], schur, couplings


def solution(mesh):
    placed = (
        P("tile", None, None),
        P("tile"),
        P("tile", "layer", None, None),
        P("tile", "layer", None),
    )
    return jax.shard_map(
        functools.partial(body, mesh.shape["tile"], mesh.shape["layer"]),
        mesh=mesh,
        in_specs=placed,
        out_specs=(
            P(None, "layer", None),
            P(),
            P("tile", "layer", None),
            P("tile", "layer", None, None),
        ),
        check_vma=False,
    )
```

```python
import functools

import jax
import jax.numpy as jnp
from jax import lax
from jax.experimental import pallas as pl
from jax.experimental.pallas import tpu as pltpu
from jax.sharding import PartitionSpec as P

B = 128
S = 8
NEAR = 2
HOP = 96
CHAIN, SPLIT, DIRECT = range(3)


def split(a):
    high = a.astype(jnp.bfloat16)
    return high, (a - high.astype(jnp.float32)).astype(jnp.bfloat16)


def three(a, b, dims):
    ah, al = split(a)
    bh, bl = split(b)
    dot = functools.partial(
        lax.dot_general, dimension_numbers=(dims, ((), ())), preferred_element_type=jnp.float32
    )
    return dot(ah, bh) + (dot(ah, bl) + dot(al, bh))


def nt(a, b):
    return three(a, b, ((1,), (1,)))


def nn(a, b):
    return three(a, b, ((1,), (0,)))


def tn(a, b):
    return three(a, b, ((0,), (0,)))


def pair_nt(a, b):
    (ah, al), (bh, bl) = a, b
    dot = functools.partial(
        lax.dot_general, dimension_numbers=(((1,), (1,)), ((), ())), preferred_element_type=jnp.float32
    )
    return dot(ah, bh) + dot(jnp.concatenate([ah, al], axis=1), jnp.concatenate([bl, bh], axis=1))


def total(terms):
    while len(terms) > 1:
        terms = [
            terms[i] + terms[i + 1] if i + 1 < len(terms) else terms[i]
            for i in range(0, len(terms), 2)
        ]
    return terms[0]


def spread_lane(block, lane):
    return jnp.broadcast_to(block[:, lane : lane + 1], (S, B))


def pick_lane(block, lane):
    return jnp.take_along_axis(block, jnp.full((S, B), lane, jnp.int32), axis=1)


def spread_row(block, row):
    return jnp.broadcast_to(block[row : row + 1, :], (S, B))


def base_factor(tile_ref, upper_ref, inv_ref, aside=lambda: None, when=0, upper=False):
    groups = B // S
    sub = lax.broadcasted_iota(jnp.int32, (S, B), 0)
    lane = lax.broadcasted_iota(jnp.int32, (S, B), 1)
    left = [tile_ref[S * g : S * g + S, :] for g in range(groups)]
    for b in range(groups):
        if b == when:
            aside()
        a = left[b]
        last = b + 1 == groups
        pivots = (lane < S * b + S) & (lane >= S * b)
        q = jnp.where(pivots, jnp.where(lane == sub + S * b, 1.0, 0.0), a)
        cols = [pick_lane(a, S * b + j) for j in range(S)]
        e = [[spread_row(cols[j], i) if j <= i else None for j in range(S)] for i in range(S)]
        rq = [spread_row(q, i) for i in range(S)]
        ra = [spread_row(a, i) for i in range(S)] if upper else []
        near = [] if last else [spread_lane(left[b + 1], S * b + j) for j in range(S)]
        inv, root = [None] * S, [None] * S
        low = [[None] * S for _ in range(S)]

        def eliminate(rows, i, j):
            rows[i] = rows[i] - low[i][j] * rows[j]

        for p in range(0, S, 2):
            top, mid, end = e[p][p], e[p + 1][p], e[p + 1][p + 1]
            det = top * end - mid * mid
            inv[p] = 1.0 / top
            rdet = 1.0 / det
            inv[p + 1] = top * rdet
            root[p], root[p + 1] = lax.rsqrt(top), lax.rsqrt(det * inv[p])
            low[p + 1][p] = mid * inv[p]
            tail = range(p + 2, S)
            cross = {i: top * e[i][p + 1] - mid * e[i][p] for i in tail}
            scaled = {i: cross[i] * inv[p] for i in tail}
            for i in tail:
                low[i][p] = e[i][p] * inv[p]
                low[i][p + 1] = cross[i] * rdet
            for k in tail:
                for i in range(k, S):
                    kept = e[i][k] - low[i][p] * e[k][p]
                    e[i][k] = kept - (cross[i] * scaled[k]) * rdet
            for j in (p, p + 1):
                for i in range(j + 1, S):
                    eliminate(rq, i, j)
                    if upper:
                        eliminate(ra, i, j)
                    if near:
                        eliminate(near, i, j)
        xq = None
        for j in range(S):
            yq = rq[j] * root[j]
            xq = yq if xq is None else jnp.where(sub == j, yq, xq)
        if upper:
            xa = None
            for j in range(S):
                ya = ra[j] * root[j]
                xa = ya if xa is None else jnp.where(sub == j, ya, xa)
            upper_ref[S * b : S * b + S, :] = jnp.where(lane >= sub + S * b, xa, 0.0)
        inv_ref[S * b : S * b + S, :] = jnp.where(lane < S * b + S, xq, 0.0)
        if last:
            break
        w = [rq[j] * inv[j] for j in range(S)]
        rest = jnp.where(pivots, 0.0, left[b + 1])
        for j in range(S):
            rest = rest - near[j] * w[j]
        left[b + 1] = rest
        if b + 2 == groups:
            continue
        for i in range(S - 1, 0, -1):
            for j in range(i):
                w[j] = w[j] - low[i][j] * w[i]
        for g in range(b + 2, min(b + 1 + NEAR, groups)):
            m = [spread_lane(left[g], S * b + j) for j in range(S)]
            left[g] = jnp.where(pivots, 0.0, left[g]) - total([m[j] * w[j] for j in range(S)])
        far = b + 1 + NEAR
        if far < groups:
            packed = w[0]
            for j in range(1, S):
                packed = jnp.where(sub == j, w[j], packed)
            rows = [packed if g == b else jnp.zeros((S, B), jnp.float32) for g in range(groups)]
            moved = nn(jnp.concatenate(left[far:], axis=0), jnp.concatenate(rows, axis=0))
            for g in range(far, groups):
                at = S * (g - far)
                left[g] = jnp.where(pivots, 0.0, left[g]) - moved[at : at + S, :]


def panel_kernel(
    tiles, layers, diag_ref, basis_ref, ranks_ref, cores_ref,
    factor_ref, z_ref, diag_out, cores_out,
    work, low, low_h, low_l, inv_h, inv_l, z_h, z_l, z_rest, corr, block, upper, inverse, masked_t, col, oth, w_rows, w_cols, gram,
    local, recv_work, send_work, recv_low, send_low, recv_z, send_z,
    recvc, sendc, recvo, sendo,
):
    t = lax.axis_index("tile")
    l = lax.axis_index("layer")
    rows, order = diag_ref.shape[1], diag_ref.shape[2]
    rmax = basis_ref.shape[0]
    panels = order // B
    early = order - B
    span = cores_ref.shape[1]
    half = tiles // 2
    hub = (t == 0) & (l == 0)
    spoke = jnp.logical_not(hub)
    fan = ((t == 0) & (l > 0)) | ((t == 1) & (l == 0))
    side = (t % 2 == 0) & spoke

    def remote(src, dst, send, recv, to_t, to_l):
        return pltpu.make_async_remote_copy(
            src_ref=src, dst_ref=dst, send_sem=send, recv_sem=recv,
            device_id=(to_t, to_l), device_id_type=pl.DeviceIdType.MESH,
        )

    def each(count, act):
        lax.fori_loop(0, count, lambda i, c: (act(i), c)[1], 0)

    def needed(j, piece):
        return (piece + 1) * rows > j * B

    def parcels(piece):
        top, end = piece * rows, (piece + 1) * rows
        wide = min(2 * B, order)
        cuts = [(0, B, 0, B), (B, 2 * B, 0, wide), (2 * B, 3 * B, 0, wide), (3 * B, order, 0, wide)]
        cuts += [(j * B, order, j * B, j * B + B) for j in range(2, panels)]
        found = []
        for tag, (r0, r1, c0, c1) in enumerate(cuts):
            r0, r1 = max(r0, top), min(r1, end)
            if r0 < r1:
                found.append((tag, r0, r1, c0, c1))
        return found

    def gathered(piece, tag, r0, r1, c0, c1):
        return remote(
            diag_ref.at[0, r0 - piece * rows : r1 - piece * rows, c0:c1], work.at[r0:r1, c0:c1],
            send_work.at[tag], recv_work.at[piece, tag], 0, 0,
        )

    def kept(tag, r0, r1, c0, c1):
        return pltpu.make_async_copy(
            diag_ref.at[0, r0:r1, c0:c1], work.at[r0:r1, c0:c1], recv_work.at[0, tag]
        )

    def parts(k, piece, far):
        top, end = piece * rows, (piece + 1) * rows
        r0, r1 = ((k + 2) * B, order) if far else (k * B, (k + 2) * B)
        r0, r1 = max(r0, top), min(r1, end)
        cuts = [r0 - top + HOP * i for i in range(pl.cdiv(max(r1 - r0, 0), HOP))]
        return [(2 * far + i, r, min(r + HOP, r1 - top)) for i, r in enumerate(cuts)]

    def down_low(k, part, to_t, child):
        tag, r0, r1 = part
        piece = factor_ref.at[0, r0:r1, k * B : k * B + B]
        return remote(
            piece, piece, send_low.at[k, tag, child], recv_low.at[k, tag], to_t, l
        )

    def out_low(k, part, piece):
        tag, r0, r1 = part
        return remote(
            low.at[piece * rows + r0 : piece * rows + r1, k * B : k * B + B],
            factor_ref.at[0, r0:r1, k * B : k * B + B],
            send_low.at[k, tag, piece], recv_low.at[k, tag], 0 if piece else 1, piece,
        )

    edges = (0, panels // 2 * B, early, order)

    ships = [[] for _ in range(panels)]
    ships[1] = [(True, 0, False), (True, 1, False)]
    ships[2] = [(True, 0, True), (True, 1, True), (True, 2, False)]
    for k in range(3, panels):
        ships[k] = [(True, k - 1, True), (True, k, False)]
    ships[panels // 2 - 1].append((False, 0, False))
    ships[panels - 2].insert(1, (False, 1, False))
    ships[panels - 1] = [(False, 2, False), (True, panels - 1, False)]

    def z_part(part):
        return z_ref.at[:, edges[part] : edges[part + 1]]

    def out_z(part, piece):
        return remote(
            z_part(part), z_part(part), send_z.at[part, piece], recv_z.at[part],
            0 if piece else 1, piece,
        )

    def down_z(part, to_t, child):
        return remote(z_part(part), z_part(part), send_z.at[part, child], recv_z.at[part], to_t, l)

    def route(k):
        return DIRECT if k + 1 == panels else SPLIT if k + 2 == panels else CHAIN

    def onward(copy, act, way):
        @pl.when(fan)
        def _():
            if way == DIRECT:
                each(half - 1, lambda i: act(copy(2 * (half - 1 - i), half - 1 - i)))
            else:
                if way == SPLIT and half > 2:
                    act(copy(tiles - 2, 2))
                act(copy(2, 1))

        if way != DIRECT:
            reach = 4 if way == SPLIT and half > 2 else 2

            @pl.when((t > 1) & (t % 2 == 0) & (t + reach < tiles))
            def _():
                act(copy(t + 2, 1))

        @pl.when(side)
        def _():
            act(copy(t + 1, 0))

    def start(copy):
        copy.start()

    def sent(copy):
        copy.wait_send()

    def column_to(to_l):
        return remote(cores_ref.at[0, 0], col, sendc.at[to_l], recvc, t, to_l)

    def column_kept():
        return pltpu.make_async_copy(cores_ref.at[0, 0], col, recvc)

    def other_to(to_t):
        return remote(
            cores_ref.at[0, 0], oth.at[t % span], sendo.at[to_t], recvo.at[t % span], to_t, t // span
        )

    def other_kept():
        return pltpu.make_async_copy(cores_ref.at[0, 0], oth.at[t % span], recvo.at[t % span])

    basis_in = pltpu.make_async_copy(basis_ref, masked_t, local.at[0])
    diag_in = pltpu.make_async_copy(diag_ref, diag_out, local.at[1])
    cores_in = pltpu.make_async_copy(cores_ref, cores_out, local.at[2])

    def mask():
        basis_in.wait()
        row = lax.broadcasted_iota(jnp.int32, (rmax, order), 0)
        masked_t[...] = masked_t[...] * jnp.where(row < ranks_ref[0], 1.0, 0.0)

    barrier = pltpu.get_barrier_semaphore()
    devices = tiles * layers

    @pl.when(hub)
    def _():
        for parcel in parcels(0):
            kept(*parcel).start()
        basis_in.start()

        def greet(i):
            pl.semaphore_signal(
                barrier, inc=1, device_id=((i + 1) // layers, (i + 1) % layers),
                device_id_type=pl.DeviceIdType.MESH,
            )

        each(devices - 1, greet)

    @pl.when(spoke)
    def _():
        factor_ref[...] = jnp.zeros_like(factor_ref)
        pl.semaphore_signal(barrier, inc=1, device_id=(0, 0), device_id_type=pl.DeviceIdType.MESH)
        pl.semaphore_wait(barrier, 1)

    def gather(step):
        for piece in range(1, layers):
            moves = parcels(piece)
            now = [(m, True) for m in moves[step : step + 1]]
            if step > 1:
                now = [(m, False) for m in moves[step - 2 : step - 1]] + now
            if now:
                @pl.when((t == 0) & (l == piece))
                def _():
                    for move, begin in now:
                        copy = gathered(piece, *move)
                        copy.start() if begin else copy.wait_send()

    for step in range(panels + 2):
        gather(step)

    diag_in.start()
    cores_in.start()

    def land(piece, parcel):
        if piece:
            gathered(piece, *parcel).wait_recv()
        else:
            kept(*parcel).wait()

    def arrived(tag, block_row=None):
        for piece in range(layers):
            for parcel in parcels(piece):
                if parcel[0] != tag:
                    continue
                near = block_row is None or (
                    piece * rows < (block_row + 1) * B and (piece + 1) * rows > block_row * B
                )
                yield near, functools.partial(land, piece, parcel)

    def await_near(tag, block_row):
        for near, wait in arrived(tag, block_row):
            if near:
                wait()

    def await_far(tag, block_row):
        for near, wait in arrived(tag, block_row):
            if not near:
                wait()

    def await_all(tag):
        for _, wait in arrived(tag):
            wait()

    def span_of(first, last):
        return slice(first * B, last * B)

    def halves(r, c):
        return low_h[r, c], low_l[r, c]

    def put(r, c, value):
        low[r, c] = value
        low_h[r, c], low_l[r, c] = split(value)

    def inverse_of(k):
        return inv_h[k], inv_l[k]

    def catch_up(k, first, last):
        r = span_of(first, last)
        done, here = span_of(k - 1, k), span_of(k, k + 1)
        put(r, done, pair_nt(split(work[r, done]), inverse_of(k - 1)))
        before = span_of(0, k)
        work[r, here] = work[r, here] - pair_nt(halves(r, before), halves(here, before))

    def stage(k):
        here, following = span_of(k, k + 1), span_of(k + 1, k + 2)

        def aside():
            if k == 1:
                await_all(2)
            if k == 2:
                await_all(3)
                catch_up(1, 3, panels)
            if k > 1:
                await_far(k + 2, k)
            before = span_of(0, k)
            z_rest[...] = masked_t[:, here] - pair_nt(
                (z_h[:, before], z_l[:, before]), halves(here, before)
            )
            if k + 1 < panels:
                catch_up(k, k + 1, k + 2 if k == 1 else panels)
                corr[...] = pair_nt(halves(following, before), halves(following, before))

        if k:
            base_factor(
                block, upper, inverse, aside, B // S // 2 if k < 3 else 0, k + 1 == panels
            )
        else:
            base_factor(block, upper, inverse)

    def settle(k):
        here, following = span_of(k, k + 1), span_of(k + 1, k + 2)
        inv = split(inverse[...])
        inv_h[k], inv_l[k] = inv
        if k + 1 == panels:
            low[here, here] = upper[...].T
        else:
            row = lax.broadcasted_iota(jnp.int32, (B, B), 0)
            column = lax.broadcasted_iota(jnp.int32, (B, B), 1)
            own = pair_nt(split(block[...]), inv)
            put(here, here, jnp.where(row >= column, own, 0.0))
        if k + 1 < panels:
            below = pair_nt(split(work[following, here]), inv)
            put(following, here, below)
            parts_of = split(below)
            rest = work[following, following] - pair_nt(parts_of, parts_of)
            block[...] = rest - corr[...] if k else rest
        part = z_rest[...] if k else masked_t[:, here]
        solved = pair_nt(split(part), inv)
        z_ref[:, here] = solved
        z_h[:, here], z_l[:, here] = split(solved)

    def ship_low(c, far):
        for piece in range(layers):
            for part in parts(c, piece, far):
                out_low(c, part, piece).start()

    def ship_z(part):
        for piece in range(layers):
            out_z(part, piece).start()

    @pl.when(hub)
    def _():
        await_all(0)
        block[...] = work[:B, :B]
        for k in range(panels):
            stage(k)
            if k == 0:
                mask()
                await_all(1)
            elif k + 1 < panels:
                await_near(k + 3, k + 1)
            settle(k)
            if k == 1:
                pl.semaphore_wait(barrier, devices - 1)
            for act, c, far in ships[k]:
                if act:
                    ship_low(c, far)
                else:
                    ship_z(c)
        factor_ref[...] = jnp.zeros_like(factor_ref)
        for c in range(panels):
            r0, r1 = c * B, min(rows, order)
            if r0 < r1:
                factor_ref[0, r0:r1, c * B : c * B + B] = low[r0:r1, c * B : c * B + B]

    @pl.when(spoke)
    def _():
        basis_in.start()

        def relay(k, far):
            for piece in range(layers):
                found = parts(k, piece, far)
                if found:
                    @pl.when(l == piece)
                    def _():
                        for part in found:
                            down_low(k, part, t, 0).wait_recv()
                            onward(functools.partial(down_low, k, part), start, route(k))

        def relay_z(part):
            down_z(part, t, 0).wait_recv()
            onward(functools.partial(down_z, part), start, DIRECT)

        relay(0, False)

        @pl.when(t > 0)
        def _():
            @pl.when(l == 0)
            def _():
                each(layers - 1, lambda i: column_to(i + 1).start())
                column_kept().start()

                def other(i):
                    to_t = 1 + lax.rem(t - 1 + i, tiles - 1)
                    pl.when((to_t != t) | (t // span != 0))(lambda: other_to(to_t).start())

                each(tiles - 1, other)
                pl.when(t // span == 0)(lambda: other_kept().start())

        relay(1, False)

        @pl.when(t > 0)
        def _():
            pl.when(l == 0)(lambda: column_kept().wait())
            pl.when(l != 0)(lambda: column_to(0).wait_recv())

            def take_other(s):
                mine = (l == 0) & (l * span + s == t)

                @pl.when(mine)
                def _():
                    pltpu.make_async_copy(cores_ref.at[0, 0], oth.at[s], recvo.at[s]).wait()

                @pl.when(jnp.logical_not(mine) & (l * span + s > 0))
                def _():
                    remote(cores_ref.at[0, 0], oth.at[s], sendo.at[0], recvo.at[s], t, l).wait_recv()

            each(span, take_other)
            mask()
            w_cols[...] = tn(col[...], masked_t[...])
            own = masked_t[...].T
            w_rows[...] = nn(own, col[...])

        for k in range(2, panels):
            for act, c, far in ships[k]:
                if act:
                    relay(c, far)
                else:
                    if c == 2:
                        gram[...] = nt(z_ref[:, :early], z_ref[:, :early])
                    relay_z(c)

        @pl.when(t == 0)
        def _():
            basis_in.wait()

        for step in range(panels + 2, panels + 4):
            gather(step)

    diag_in.wait()
    cores_in.wait()

    @pl.when(t > 0)
    def _():
        mine = pl.ds(pl.multiple_of(l * rows, S), rows)
        square = gram[...] + nt(z_ref[:, early:], z_ref[:, early:])
        partial = nn(w_rows[mine, :], square)
        diag_out[0] = diag_out[0] - nn(partial, w_cols[...])
        coef = nn(col[...], square)
        for s in range(span):
            other_id = l * span + s

            @pl.when((t > other_id) & (other_id > 0))
            def _():
                cores_out[0, s] = cores_out[0, s] - nt(coef, oth[s])

    @pl.when(hub)
    def _():
        for c in range(panels):
            for piece in range(layers):
                for part in parts(c, piece, False) + parts(c, piece, True):
                    out_low(c, part, piece).wait_send()
        for part in range(3):
            for piece in range(layers):
                out_z(part, piece).wait_send()

    @pl.when(spoke)
    def _():
        for piece in range(layers):
            @pl.when(l == piece)
            def _():
                for k in range(panels):
                    for part in parts(k, piece, False) + parts(k, piece, True):
                        onward(functools.partial(down_low, k, part), sent, route(k))
        for part in range(3):
            onward(functools.partial(down_z, part), sent, DIRECT)

    @pl.when((l == 0) & (t > 0))
    def _():
        each(layers - 1, lambda i: column_to(i + 1).wait_send())

        def other(i):
            to_t = 1 + lax.rem(t - 1 + i, tiles - 1)
            pl.when((to_t != t) | (t // span != 0))(lambda: other_to(to_t).wait_send())

        each(tiles - 1, other)


def emit_kernel(a, b, c, d, a_out, b_out, c_out, d_out, sems):
    copies = [
        pltpu.make_async_copy(src, dst, sems.at[i])
        for i, (src, dst) in enumerate(((a, a_out), (c, c_out), (b, b_out), (d, d_out)))
    ]
    for copy in copies:
        copy.start()
    for copy in copies:
        copy.wait()


def fixed(x):
    return pltpu.with_memory_space_constraint(x, pltpu.HBM)


def body(tiles, layers, basis, ranks, cores, diag):
    rmax = basis.shape[2]
    span = cores.shape[1]
    rows, order = diag.shape[1], diag.shape[2]
    panels = order // B
    vm = pl.BlockSpec(memory_space=pltpu.VMEM)
    hbm = pl.BlockSpec(memory_space=pl.ANY)
    f32, bf16 = jnp.float32, jnp.bfloat16
    dma = pltpu.SemaphoreType.DMA
    shapes = ((1, rows, order), (rmax, order), diag.shape, cores.shape)
    children = max(layers, tiles // 2)
    results = pl.pallas_call(
        functools.partial(panel_kernel, tiles, layers),
        out_shape=tuple(pltpu.VMEM(shape, f32) for shape in shapes),
        in_specs=[hbm, hbm, pl.BlockSpec(memory_space=pltpu.SMEM), hbm],
        out_specs=(vm,) * 4,
        scratch_shapes=[
            pltpu.VMEM((order, order), f32),
            pltpu.VMEM((order, order), f32),
            pltpu.VMEM((order, order), bf16),
            pltpu.VMEM((order, order), bf16),
            pltpu.VMEM((panels, B, B), bf16),
            pltpu.VMEM((panels, B, B), bf16),
            pltpu.VMEM((rmax, order), bf16),
            pltpu.VMEM((rmax, order), bf16),
            pltpu.VMEM((rmax, B), f32),
            pltpu.VMEM((B, B), f32),
            pltpu.VMEM((B, B), f32),
            pltpu.VMEM((B, B), f32),
            pltpu.VMEM((B, B), f32),
            pltpu.VMEM((rmax, order), f32),
            pltpu.VMEM((rmax, rmax), f32),
            pltpu.VMEM((span, rmax, rmax), f32),
            pltpu.VMEM((order, rmax), f32),
            pltpu.VMEM((rmax, order), f32),
            pltpu.VMEM((rmax, rmax), f32),
            dma((3,)),
            dma((layers, panels + 2)),
            dma((panels + 2,)),
            dma((panels, 4)),
            dma((panels, 4, children)),
            dma((3,)),
            dma((3, children)),
            dma,
            dma((layers,)),
            dma((span,)),
            dma((tiles,)),
        ],
        compiler_params=pltpu.CompilerParams(
            collective_id=0, has_side_effects=True, vmem_limit_bytes=24 << 20,
        ),
    )(fixed(diag), fixed(basis[0].T), ranks, fixed(cores))
    factors, zt, schur, couplings = pl.pallas_call(
        emit_kernel,
        out_shape=tuple(jax.ShapeDtypeStruct(shape, f32) for shape in shapes),
        in_specs=[vm] * 4,
        out_specs=(hbm,) * 4,
        scratch_shapes=[dma((4,))],
        compiler_params=pltpu.CompilerParams(vmem_limit_bytes=1 << 20),
    )(*results)
    return factors, zt.T[None], schur, couplings


def solution(mesh):
    placed = (
        P("tile", None, None),
        P("tile"),
        P("tile", "layer", None, None),
        P("tile", "layer", None),
    )
    return jax.shard_map(
        functools.partial(body, mesh.shape["tile"], mesh.shape["layer"]),
        mesh=mesh,
        in_specs=placed,
        out_specs=(
            P(None, "layer", None),
            P(),
            P("tile", "layer", None),
            P("tile", "layer", None, None),
        ),
        check_vma=False,
    )
```

```python
import functools

import jax
import jax.numpy as jnp
from jax import lax
from jax.experimental import pallas as pl
from jax.experimental.pallas import tpu as pltpu
from jax.sharding import PartitionSpec as P

B = 128
S = 8
NEAR = 2
HOP = 96
CHAIN, SPLIT, DIRECT = range(3)


def split(a):
    high = a.astype(jnp.bfloat16)
    return high, (a - high.astype(jnp.float32)).astype(jnp.bfloat16)


def three(a, b, dims):
    ah, al = split(a)
    bh, bl = split(b)
    dot = functools.partial(
        lax.dot_general, dimension_numbers=(dims, ((), ())), preferred_element_type=jnp.float32
    )
    return dot(ah, bh) + (dot(ah, bl) + dot(al, bh))


def nt(a, b):
    return three(a, b, ((1,), (1,)))


def nn(a, b):
    return three(a, b, ((1,), (0,)))


def tn(a, b):
    return three(a, b, ((0,), (0,)))


def pair_nt(a, b):
    (ah, al), (bh, bl) = a, b
    dot = functools.partial(
        lax.dot_general, dimension_numbers=(((1,), (1,)), ((), ())), preferred_element_type=jnp.float32
    )
    return dot(ah, bh) + dot(jnp.concatenate([ah, al], axis=1), jnp.concatenate([bl, bh], axis=1))


def total(terms):
    while len(terms) > 1:
        terms = [
            terms[i] + terms[i + 1] if i + 1 < len(terms) else terms[i]
            for i in range(0, len(terms), 2)
        ]
    return terms[0]


def spread_lane(block, lane):
    return jnp.broadcast_to(block[:, lane : lane + 1], (S, B))


def pick_lane(block, lane):
    return jnp.take_along_axis(block, jnp.full((S, B), lane, jnp.int32), axis=1)


def spread_row(block, row):
    return jnp.broadcast_to(block[row : row + 1, :], (S, B))


def base_factor(tile_ref, upper_ref, inv_ref, aside=lambda: None, when=0, upper=False):
    groups = B // S
    sub = lax.broadcasted_iota(jnp.int32, (S, B), 0)
    lane = lax.broadcasted_iota(jnp.int32, (S, B), 1)
    left = [tile_ref[S * g : S * g + S, :] for g in range(groups)]
    for b in range(groups):
        if b == when:
            aside()
        a = left[b]
        last = b + 1 == groups
        pivots = (lane < S * b + S) & (lane >= S * b)
        q = jnp.where(pivots, jnp.where(lane == sub + S * b, 1.0, 0.0), a)
        cols = [pick_lane(a, S * b + j) for j in range(S)]
        e = [[spread_row(cols[j], i) if j <= i else None for j in range(S)] for i in range(S)]
        rq = [spread_row(q, i) for i in range(S)]
        ra = [spread_row(a, i) for i in range(S)] if upper else []
        near = [] if last else [spread_lane(left[b + 1], S * b + j) for j in range(S)]
        inv, root = [None] * S, [None] * S
        low = [[None] * S for _ in range(S)]

        def eliminate(rows, i, j):
            rows[i] = rows[i] - low[i][j] * rows[j]

        for p in range(0, S, 2):
            top, mid, end = e[p][p], e[p + 1][p], e[p + 1][p + 1]
            det = top * end - mid * mid
            inv[p] = 1.0 / top
            rdet = 1.0 / det
            inv[p + 1] = top * rdet
            root[p], root[p + 1] = lax.rsqrt(top), lax.rsqrt(det * inv[p])
            low[p + 1][p] = mid * inv[p]
            tail = range(p + 2, S)
            cross = {i: top * e[i][p + 1] - mid * e[i][p] for i in tail}
            scaled = {i: cross[i] * inv[p] for i in tail}
            for i in tail:
                low[i][p] = e[i][p] * inv[p]
                low[i][p + 1] = cross[i] * rdet
            for k in tail:
                for i in range(k, S):
                    kept = e[i][k] - low[i][p] * e[k][p]
                    e[i][k] = kept - (cross[i] * scaled[k]) * rdet
            for j in (p, p + 1):
                for i in range(j + 1, S):
                    eliminate(rq, i, j)
                    if upper:
                        eliminate(ra, i, j)
                    if near:
                        eliminate(near, i, j)
        xq = None
        for j in range(S):
            yq = rq[j] * root[j]
            xq = yq if xq is None else jnp.where(sub == j, yq, xq)
        if upper:
            xa = None
            for j in range(S):
                ya = ra[j] * root[j]
                xa = ya if xa is None else jnp.where(sub == j, ya, xa)
            upper_ref[S * b : S * b + S, :] = jnp.where(lane >= sub + S * b, xa, 0.0)
        inv_ref[S * b : S * b + S, :] = jnp.where(lane < S * b + S, xq, 0.0)
        if last:
            break
        w = [rq[j] * inv[j] for j in range(S)]
        rest = jnp.where(pivots, 0.0, left[b + 1])
        for j in range(S):
            rest = rest - near[j] * w[j]
        left[b + 1] = rest
        if b + 2 == groups:
            continue
        for i in range(S - 1, 0, -1):
            for j in range(i):
                w[j] = w[j] - low[i][j] * w[i]
        for g in range(b + 2, min(b + 1 + NEAR, groups)):
            m = [spread_lane(left[g], S * b + j) for j in range(S)]
            left[g] = jnp.where(pivots, 0.0, left[g]) - total([m[j] * w[j] for j in range(S)])
        far = b + 1 + NEAR
        if far < groups:
            packed = w[0]
            for j in range(1, S):
                packed = jnp.where(sub == j, w[j], packed)
            rows = [packed if g == b else jnp.zeros((S, B), jnp.float32) for g in range(groups)]
            moved = nn(jnp.concatenate(left[far:], axis=0), jnp.concatenate(rows, axis=0))
            for g in range(far, groups):
                at = S * (g - far)
                left[g] = jnp.where(pivots, 0.0, left[g]) - moved[at : at + S, :]


def panel_kernel(
    tiles, layers, diag_ref, basis_ref, ranks_ref, cores_ref,
    factor_ref, z_ref, diag_out, cores_out,
    work, low, low_h, low_l, inv_h, inv_l, z_h, z_l, z_rest, corr, block, upper, inverse, masked_t, col, oth, w_rows, w_cols, gram,
    local, recv_work, send_work, recv_low, send_low, recv_z, send_z,
    recvc, sendc, recvo, sendo,
):
    t = lax.axis_index("tile")
    l = lax.axis_index("layer")
    rows, order = diag_ref.shape[1], diag_ref.shape[2]
    rmax = basis_ref.shape[0]
    panels = order // B
    early = order - B
    span = cores_ref.shape[1]
    half = tiles // 2
    hub = (t == 0) & (l == 0)
    spoke = jnp.logical_not(hub)
    fan = ((t == 0) & (l > 0)) | ((t == 1) & (l == 0))
    side = (t % 2 == 0) & spoke

    def remote(src, dst, send, recv, to_t, to_l):
        return pltpu.make_async_remote_copy(
            src_ref=src, dst_ref=dst, send_sem=send, recv_sem=recv,
            device_id=(to_t, to_l), device_id_type=pl.DeviceIdType.MESH,
        )

    def each(count, act):
        lax.fori_loop(0, count, lambda i, c: (act(i), c)[1], 0)

    def needed(j, piece):
        return (piece + 1) * rows > j * B

    def parcels(piece):
        top, end = piece * rows, (piece + 1) * rows
        wide = min(2 * B, order)
        cuts = [(0, B, 0, B), (B, 2 * B, 0, wide), (2 * B, 3 * B, 0, wide), (3 * B, order, 0, wide)]
        cuts += [(j * B, order, j * B, j * B + B) for j in range(2, panels)]
        found = []
        for tag, (r0, r1, c0, c1) in enumerate(cuts):
            r0, r1 = max(r0, top), min(r1, end)
            if r0 < r1:
                found.append((tag, r0, r1, c0, c1))
        return found

    def gathered(piece, tag, r0, r1, c0, c1):
        return remote(
            diag_ref.at[0, r0 - piece * rows : r1 - piece * rows, c0:c1], work.at[r0:r1, c0:c1],
            send_work.at[tag], recv_work.at[piece, tag], 0, 0,
        )

    def kept(tag, r0, r1, c0, c1):
        return pltpu.make_async_copy(
            diag_ref.at[0, r0:r1, c0:c1], work.at[r0:r1, c0:c1], recv_work.at[0, tag]
        )

    def parts(k, piece, far):
        top, end = piece * rows, (piece + 1) * rows
        r0, r1 = ((k + 2) * B, order) if far else (k * B, (k + 2) * B)
        r0, r1 = max(r0, top), min(r1, end)
        cuts = [r0 - top + HOP * i for i in range(pl.cdiv(max(r1 - r0, 0), HOP))]
        return [(2 * far + i, r, min(r + HOP, r1 - top)) for i, r in enumerate(cuts)]

    def down_low(k, part, to_t, child):
        tag, r0, r1 = part
        piece = factor_ref.at[0, r0:r1, k * B : k * B + B]
        return remote(
            piece, piece, send_low.at[k, tag, child], recv_low.at[k, tag], to_t, l
        )

    def out_low(k, part, piece):
        tag, r0, r1 = part
        return remote(
            low.at[piece * rows + r0 : piece * rows + r1, k * B : k * B + B],
            factor_ref.at[0, r0:r1, k * B : k * B + B],
            send_low.at[k, tag, piece], recv_low.at[k, tag], 0 if piece else 1, piece,
        )

    edges = (0, panels // 2 * B, early, order)

    ships = [[] for _ in range(panels)]
    ships[1] = [(True, 0, False), (True, 1, False)]
    ships[2] = [(True, 0, True), (True, 1, True), (True, 2, False)]
    for k in range(3, panels):
        ships[k] = [(True, k - 1, True), (True, k, False)]
    ships[panels // 2 - 1].append((False, 0, False))
    ships[panels - 2].insert(1, (False, 1, False))
    ships[panels - 1] = [(False, 2, False), (True, panels - 1, False)]

    def z_part(part):
        return z_ref.at[:, edges[part] : edges[part + 1]]

    def out_z(part, piece):
        return remote(
            z_part(part), z_part(part), send_z.at[part, piece], recv_z.at[part],
            0 if piece else 1, piece,
        )

    def down_z(part, to_t, child):
        return remote(z_part(part), z_part(part), send_z.at[part, child], recv_z.at[part], to_t, l)

    def route(k):
        return DIRECT if k + 1 == panels else SPLIT if k + 2 == panels else CHAIN

    def onward(copy, act, way):
        @pl.when(fan)
        def _():
            if way == DIRECT:
                each(half - 1, lambda i: act(copy(2 * (half - 1 - i), half - 1 - i)))
            else:
                if way == SPLIT and half > 2:
                    act(copy(tiles - 2, 2))
                act(copy(2, 1))

        if way != DIRECT:
            reach = 4 if way == SPLIT and half > 2 else 2

            @pl.when((t > 1) & (t % 2 == 0) & (t + reach < tiles))
            def _():
                act(copy(t + 2, 1))

        @pl.when(side)
        def _():
            act(copy(t + 1, 0))

    def start(copy):
        copy.start()

    def sent(copy):
        copy.wait_send()

    def column_to(to_l):
        return remote(cores_ref.at[0, 0], col, sendc.at[to_l], recvc, t, to_l)

    def column_kept():
        return pltpu.make_async_copy(cores_ref.at[0, 0], col, recvc)

    def other_to(to_t):
        return remote(
            cores_ref.at[0, 0], oth.at[t % span], sendo.at[to_t], recvo.at[t % span], to_t, t // span
        )

    def other_kept():
        return pltpu.make_async_copy(cores_ref.at[0, 0], oth.at[t % span], recvo.at[t % span])

    basis_in = pltpu.make_async_copy(basis_ref, masked_t, local.at[0])
    diag_in = pltpu.make_async_copy(diag_ref, diag_out, local.at[1])
    cores_in = pltpu.make_async_copy(cores_ref, cores_out, local.at[2])

    def mask():
        basis_in.wait()
        row = lax.broadcasted_iota(jnp.int32, (rmax, order), 0)
        masked_t[...] = masked_t[...] * jnp.where(row < ranks_ref[0], 1.0, 0.0)

    barrier = pltpu.get_barrier_semaphore()
    devices = tiles * layers

    @pl.when(hub)
    def _():
        for parcel in parcels(0):
            kept(*parcel).start()
        basis_in.start()

        def greet(i):
            pl.semaphore_signal(
                barrier, inc=1, device_id=((i + 1) // layers, (i + 1) % layers),
                device_id_type=pl.DeviceIdType.MESH,
            )

        each(devices - 1, greet)

    @pl.when(spoke)
    def _():
        factor_ref[...] = jnp.zeros_like(factor_ref)
        pl.semaphore_signal(barrier, inc=1, device_id=(0, 0), device_id_type=pl.DeviceIdType.MESH)
        pl.semaphore_wait(barrier, 1)

    def gather(step):
        for piece in range(1, layers):
            moves = parcels(piece)
            now = [(m, True) for m in moves[step : step + 1]]
            if step > 1:
                now = [(m, False) for m in moves[step - 2 : step - 1]] + now
            if now:
                @pl.when((t == 0) & (l == piece))
                def _():
                    for move, begin in now:
                        copy = gathered(piece, *move)
                        copy.start() if begin else copy.wait_send()

    for step in range(panels + 2):
        gather(step)

    diag_in.start()
    cores_in.start()

    def land(piece, parcel):
        if piece:
            gathered(piece, *parcel).wait_recv()
        else:
            kept(*parcel).wait()

    def arrived(tag, block_row=None):
        for piece in range(layers):
            for parcel in parcels(piece):
                if parcel[0] != tag:
                    continue
                near = block_row is None or (
                    piece * rows < (block_row + 1) * B and (piece + 1) * rows > block_row * B
                )
                yield near, functools.partial(land, piece, parcel)

    def await_near(tag, block_row):
        for near, wait in arrived(tag, block_row):
            if near:
                wait()

    def await_far(tag, block_row):
        for near, wait in arrived(tag, block_row):
            if not near:
                wait()

    def await_all(tag):
        for _, wait in arrived(tag):
            wait()

    def span_of(first, last):
        return slice(first * B, last * B)

    def halves(r, c):
        return low_h[r, c], low_l[r, c]

    def put(r, c, value):
        low[r, c] = value
        low_h[r, c], low_l[r, c] = split(value)

    def inverse_of(k):
        return inv_h[k], inv_l[k]

    def catch_up(k, first, last):
        r = span_of(first, last)
        done, here = span_of(k - 1, k), span_of(k, k + 1)
        put(r, done, pair_nt(split(work[r, done]), inverse_of(k - 1)))
        before = span_of(0, k)
        work[r, here] = work[r, here] - pair_nt(halves(r, before), halves(here, before))

    def stage(k):
        here, following = span_of(k, k + 1), span_of(k + 1, k + 2)

        def aside():
            if k == 1:
                await_all(2)
            if k == 2:
                await_all(3)
                catch_up(1, 3, panels)
            if k > 1:
                await_far(k + 2, k)
            before = span_of(0, k)
            z_rest[...] = masked_t[:, here] - pair_nt(
                (z_h[:, before], z_l[:, before]), halves(here, before)
            )
            if k + 1 < panels:
                catch_up(k, k + 1, k + 2 if k == 1 else panels)
                corr[...] = pair_nt(halves(following, before), halves(following, before))

        if k:
            base_factor(
                block, upper, inverse, aside, B // S // 2 if k < 3 else 0, k + 1 == panels
            )
        else:
            base_factor(block, upper, inverse)

    def settle(k):
        here, following = span_of(k, k + 1), span_of(k + 1, k + 2)
        inv = split(inverse[...])
        inv_h[k], inv_l[k] = inv
        if k + 1 == panels:
            low[here, here] = upper[...].T
        else:
            row = lax.broadcasted_iota(jnp.int32, (B, B), 0)
            column = lax.broadcasted_iota(jnp.int32, (B, B), 1)
            own = pair_nt(split(block[...]), inv)
            put(here, here, jnp.where(row >= column, own, 0.0))
        if k + 1 < panels:
            below = pair_nt(split(work[following, here]), inv)
            put(following, here, below)
            parts_of = split(below)
            rest = work[following, following] - pair_nt(parts_of, parts_of)
            block[...] = rest - corr[...] if k else rest
        part = z_rest[...] if k else masked_t[:, here]
        solved = pair_nt(split(part), inv)
        z_ref[:, here] = solved
        z_h[:, here], z_l[:, here] = split(solved)

    def ship_low(c, far):
        for piece in range(layers):
            for part in parts(c, piece, far):
                out_low(c, part, piece).start()

    def ship_z(part):
        for piece in range(layers):
            out_z(part, piece).start()

    @pl.when(hub)
    def _():
        await_all(0)
        block[...] = work[:B, :B]
        for k in range(panels):
            stage(k)
            if k == 0:
                mask()
                await_all(1)
            elif k + 1 < panels:
                await_near(k + 3, k + 1)
            settle(k)
            if k == 1:
                pl.semaphore_wait(barrier, devices - 1)
            for act, c, far in ships[k]:
                if act:
                    ship_low(c, far)
                else:
                    ship_z(c)
        factor_ref[...] = jnp.zeros_like(factor_ref)
        for c in range(panels):
            r0, r1 = c * B, min(rows, order)
            if r0 < r1:
                factor_ref[0, r0:r1, c * B : c * B + B] = low[r0:r1, c * B : c * B + B]

    @pl.when(spoke)
    def _():
        basis_in.start()

        def relay(k, far):
            for piece in range(layers):
                found = parts(k, piece, far)
                if found:
                    @pl.when(l == piece)
                    def _():
                        for part in found:
                            down_low(k, part, t, 0).wait_recv()
                            onward(functools.partial(down_low, k, part), start, route(k))

        def relay_z(part):
            down_z(part, t, 0).wait_recv()
            onward(functools.partial(down_z, part), start, DIRECT)

        relay(0, False)

        @pl.when(t > 0)
        def _():
            @pl.when(l == 0)
            def _():
                each(layers - 1, lambda i: column_to(i + 1).start())
                column_kept().start()

                def other(i):
                    to_t = 1 + lax.rem(t - 1 + i, tiles - 1)
                    pl.when((to_t != t) | (t // span != 0))(lambda: other_to(to_t).start())

                each(tiles - 1, other)
                pl.when(t // span == 0)(lambda: other_kept().start())

        relay(1, False)

        @pl.when(t > 0)
        def _():
            pl.when(l == 0)(lambda: column_kept().wait())
            pl.when(l != 0)(lambda: column_to(0).wait_recv())

            def take_other(s):
                mine = (l == 0) & (l * span + s == t)

                @pl.when(mine)
                def _():
                    pltpu.make_async_copy(cores_ref.at[0, 0], oth.at[s], recvo.at[s]).wait()

                @pl.when(jnp.logical_not(mine) & (l * span + s > 0))
                def _():
                    remote(cores_ref.at[0, 0], oth.at[s], sendo.at[0], recvo.at[s], t, l).wait_recv()

            each(span, take_other)
            mask()
            w_cols[...] = tn(col[...], masked_t[...])
            own = masked_t[...].T
            w_rows[...] = nn(own, col[...])

        def follow(piece):
            for k in range(2, panels):
                for act, c, far in ships[k]:
                    if act:
                        for part in parts(c, piece, far):
                            down_low(c, part, t, 0).wait_recv()
                            onward(functools.partial(down_low, c, part), start, route(c))
                    else:
                        if c == 2:
                            gram[...] = nt(z_ref[:, :early], z_ref[:, :early])
                        relay_z(c)

        for piece in range(layers):
            pl.when(l == piece)(functools.partial(follow, piece))

        @pl.when(t == 0)
        def _():
            basis_in.wait()

        for step in range(panels + 2, panels + 4):
            gather(step)

    diag_in.wait()
    cores_in.wait()

    @pl.when(t > 0)
    def _():
        mine = pl.ds(pl.multiple_of(l * rows, S), rows)
        square = gram[...] + nt(z_ref[:, early:], z_ref[:, early:])
        partial = nn(w_rows[mine, :], square)
        diag_out[0] = diag_out[0] - nn(partial, w_cols[...])
        coef = nn(col[...], square)
        for s in range(span):
            other_id = l * span + s

            @pl.when((t > other_id) & (other_id > 0))
            def _():
                cores_out[0, s] = cores_out[0, s] - nt(coef, oth[s])

    @pl.when(hub)
    def _():
        for c in range(panels):
            for piece in range(layers):
                for part in parts(c, piece, False) + parts(c, piece, True):
                    out_low(c, part, piece).wait_send()
        for part in range(3):
            for piece in range(layers):
                out_z(part, piece).wait_send()

    @pl.when(spoke)
    def _():
        for piece in range(layers):
            @pl.when(l == piece)
            def _():
                for k in range(panels):
                    for part in parts(k, piece, False) + parts(k, piece, True):
                        onward(functools.partial(down_low, k, part), sent, route(k))
        for part in range(3):
            onward(functools.partial(down_z, part), sent, DIRECT)

    @pl.when((l == 0) & (t > 0))
    def _():
        each(layers - 1, lambda i: column_to(i + 1).wait_send())

        def other(i):
            to_t = 1 + lax.rem(t - 1 + i, tiles - 1)
            pl.when((to_t != t) | (t // span != 0))(lambda: other_to(to_t).wait_send())

        each(tiles - 1, other)


def emit_kernel(a, b, c, d, a_out, b_out, c_out, d_out, sems):
    copies = [
        pltpu.make_async_copy(src, dst, sems.at[i])
        for i, (src, dst) in enumerate(((a, a_out), (c, c_out), (b, b_out), (d, d_out)))
    ]
    for copy in copies:
        copy.start()
    for copy in copies:
        copy.wait()


def fixed(x):
    return pltpu.with_memory_space_constraint(x, pltpu.HBM)


def body(tiles, layers, basis, ranks, cores, diag):
    rmax = basis.shape[2]
    span = cores.shape[1]
    rows, order = diag.shape[1], diag.shape[2]
    panels = order // B
    vm = pl.BlockSpec(memory_space=pltpu.VMEM)
    hbm = pl.BlockSpec(memory_space=pl.ANY)
    f32, bf16 = jnp.float32, jnp.bfloat16
    dma = pltpu.SemaphoreType.DMA
    shapes = ((1, rows, order), (rmax, order), diag.shape, cores.shape)
    children = max(layers, tiles // 2)
    results = pl.pallas_call(
        functools.partial(panel_kernel, tiles, layers),
        out_shape=tuple(pltpu.VMEM(shape, f32) for shape in shapes),
        in_specs=[hbm, hbm, pl.BlockSpec(memory_space=pltpu.SMEM), hbm],
        out_specs=(vm,) * 4,
        scratch_shapes=[
            pltpu.VMEM((order, order), f32),
            pltpu.VMEM((order, order), f32),
            pltpu.VMEM((order, order), bf16),
            pltpu.VMEM((order, order), bf16),
            pltpu.VMEM((panels, B, B), bf16),
            pltpu.VMEM((panels, B, B), bf16),
            pltpu.VMEM((rmax, order), bf16),
            pltpu.VMEM((rmax, order), bf16),
            pltpu.VMEM((rmax, B), f32),
            pltpu.VMEM((B, B), f32),
            pltpu.VMEM((B, B), f32),
            pltpu.VMEM((B, B), f32),
            pltpu.VMEM((B, B), f32),
            pltpu.VMEM((rmax, order), f32),
            pltpu.VMEM((rmax, rmax), f32),
            pltpu.VMEM((span, rmax, rmax), f32),
            pltpu.VMEM((order, rmax), f32),
            pltpu.VMEM((rmax, order), f32),
            pltpu.VMEM((rmax, rmax), f32),
            dma((3,)),
            dma((layers, panels + 2)),
            dma((panels + 2,)),
            dma((panels, 4)),
            dma((panels, 4, children)),
            dma((3,)),
            dma((3, children)),
            dma,
            dma((layers,)),
            dma((span,)),
            dma((tiles,)),
        ],
        compiler_params=pltpu.CompilerParams(
            collective_id=0, has_side_effects=True, vmem_limit_bytes=24 << 20,
        ),
    )(fixed(diag), fixed(basis[0].T), ranks, fixed(cores))
    factors, zt, schur, couplings = pl.pallas_call(
        emit_kernel,
        out_shape=tuple(jax.ShapeDtypeStruct(shape, f32) for shape in shapes),
        in_specs=[vm] * 4,
        out_specs=(hbm,) * 4,
        scratch_shapes=[dma((4,))],
        compiler_params=pltpu.CompilerParams(vmem_limit_bytes=1 << 20),
    )(*results)
    return factors, zt.T[None], schur, couplings


def solution(mesh):
    placed = (
        P("tile", None, None),
        P("tile"),
        P("tile", "layer", None, None),
        P("tile", "layer", None),
    )
    return jax.shard_map(
        functools.partial(body, mesh.shape["tile"], mesh.shape["layer"]),
        mesh=mesh,
        in_specs=placed,
        out_specs=(
            P(None, "layer", None),
            P(),
            P("tile", "layer", None),
            P("tile", "layer", None, None),
        ),
        check_vma=False,
    )
```
